768 devices in a mesh: dp: 192 (over x, z_lo, y, core), pipe: 4 (over z_hi).
Axes of the slice: x: 4, y: 8, z: 12 (z_hi: 4, z_lo: 3; z = z_hi * 3 + z_lo), core: 2. Of those that a mesh axis runs over, the one named last changes fastest.
Arguments:
- stashed: bfloat16 [4, 4, 6144, 8192], P('pipe', None, 'dp'), may hold values from -6 to 6
- kv_grads: bfloat16 [4, 4, 6144, 2048], P('pipe', None, 'dp'), may hold values from -0.0390625 to 0.0390625
- branch_grads: bfloat16 [4, 6144, 8192], P('pipe', 'dp'), may hold values from -6 to 6
- flora_seeds: int32 [4, 2], P('pipe'), may hold values from 0 to 99999
- plan: int32 [4, 4], P('pipe'), may hold values from 0 to 3, each once within a row
Outputs:
- compressed: float32 [4, 256, 2048], P('pipe')
- section_grads: bfloat16 [4, 6144, 8192], P('pipe', 'dp')
The draws below stay inside these ranges and needn't reach their ends.
Inputs may be any that keep to these rules, and one draw needn't show every extreme that they name: `plan`: each row is a permutation of the micro-batch numbers 0 to 3.
All inputs are finite; a program needn't handle non-finite values.
Results may differ from the reference program's by a relative error of at most 0.0051.
Values may be sent and summed in bfloat16 or wider, within the bound.
A program may use at most 32 MiB of HBM per device.

```python
import math
import jax
import jax.numpy as jnp

D = 8192
KVW = 1024
R = 256
MBW = 4
TOK_MB = 32
SECTIONS = 4
TOKS = 6144
N_DP = 192


def place_ends(drawn, key, smallest, top_value):
    dims = drawn.shape
    index_at = [jax.random.randint(jax.random.fold_in(key, axis), (), 0, dims[axis]) for axis in range(len(dims))]
    drawn = drawn.at[tuple(index_at)].set(smallest)
    longest = dims.index(max(dims))
    index_at[longest] = (index_at[longest] + 1) % dims[longest]
    return drawn.at[tuple(index_at)].set(top_value)


def steps_of(own_key, shape, cuts, least, high):
    factor_of, own = 1.0, jax.random.fold_in(own_key, 6)
    for dim, blocks in cuts:
        heights = jnp.exp(jax.random.uniform(jax.random.fold_in(own, dim), (blocks,), jnp.float32, least / len(cuts), high / len(cuts)))
        factor_of = factor_of * jnp.repeat(heights, shape[dim] // blocks).reshape([-1 if axis == dim else 1 for axis in range(len(shape))])
    return factor_of


def scatter_about(key, dims, scale, most, pieces=(), kind=jnp.bfloat16):
    gain = steps_of(key, dims, pieces, -0.22, 0.18) if pieces else 1.0
    drawn = jax.random.normal(key, dims, jnp.float32) * scale * gain
    return jnp.minimum(jnp.maximum(drawn, -most), most).astype(kind)


def setup_inputs(seed: int = 0) -> dict:
    splits = jax.random.split(jax.random.key(seed), 6)
    return {
        "stashed": scatter_about(splits[0], (SECTIONS, MBW, TOKS, D), 1.0, 6.0, ((0, 4), (2, 192))),
        "kv_grads": scatter_about(splits[1], (SECTIONS, MBW, TOKS, 2 * KVW), (MBW * TOK_MB * N_DP) ** -0.5, 0.0390625, ((0, 4), (2, 192))),
        "branch_grads": scatter_about(splits[2], (SECTIONS, TOKS, D), 1.0, 6.0, ((0, 4), (1, 192))),
        "flora_seeds": place_ends(jax.random.randint(splits[3], (SECTIONS, 2), 0, 100000), jax.random.fold_in(splits[3], 1), 0, 99999).astype(jnp.int32),
        "plan": jax.vmap(lambda own: jax.random.permutation(own, MBW))(jax.random.split(splits[4], SECTIONS)).reshape((SECTIONS, MBW)).astype(jnp.int32),
    }


def projection(seed_value, row_count, col_count):
    row_index = jnp.arange(row_count, dtype=jnp.int32)[:, None]
    col_index = jnp.arange(col_count, dtype=jnp.int32)[None, :]
    hashed_one = (row_index * 1031 + col_index * 2053 + seed_value * 3 + 7) % 32749
    hashed_two = (hashed_one * hashed_one + row_index * 17 + 5) % 32749
    hashed_three = (hashed_two * hashed_two + col_index * 29 + seed_value) % 32749
    scaled = hashed_three.astype(jnp.float32) * (2.0 / 32748.0) - 1.0
    return (scaled * math.sqrt(3.0 / row_count)).astype(jnp.bfloat16)

def reference(stashed, kv_grads, branch_grads, flora_seeds, plan):
    outputs = []
    for section_num in range(SECTIONS):
        key_proj = projection(flora_seeds[section_num, 0], D, R)
        value_proj = projection(flora_seeds[section_num, 1], D, R)
        key_total = jnp.zeros((R, KVW), jnp.float32)
        value_total = jnp.zeros((R, KVW), jnp.float32)
        for slot_num in range(MBW):
            inputs = stashed[section_num, slot_num]
            kv_rows = kv_grads[section_num, plan[section_num, slot_num]]
            key_side = jnp.dot(inputs, key_proj, preferred_element_type=jnp.float32).astype(jnp.bfloat16)
            value_side = jnp.dot(inputs, value_proj, preferred_element_type=jnp.float32).astype(jnp.bfloat16)
            key_total = key_total + jnp.dot(key_side.T, kv_rows[:, :KVW], preferred_element_type=jnp.float32)
            value_total = value_total + jnp.dot(value_side.T, kv_rows[:, KVW:], preferred_element_type=jnp.float32)
        outputs.append(jnp.concatenate([key_total, value_total], axis=1))
    compressed = jnp.stack(outputs)
    running = branch_grads[SECTIONS - 1]
    chain_list = [running]
    for section_num in range(SECTIONS - 2, -1, -1):
        running = (running.astype(jnp.float32) + branch_grads[section_num].astype(jnp.float32)).astype(jnp.bfloat16)
        chain_list.append(running)
    section_grads = jnp.stack(chain_list[::-1])
    return (compressed, section_grads)
```

```python
import math

import jax
import jax.numpy as jnp
from jax import lax
from jax.experimental import pallas as pl
from jax.experimental.pallas import tpu as pltpu
from jax.sharding import PartitionSpec as P

MESH = pl.DeviceIdType.MESH
NX, NZ, NY, SECTIONS = 4, 3, 8, 4
R, D, KVW, MBW, TOK = 256, 8192, 1024, 4, 32
ROWS = MBW * TOK
MOD = 32749
RQ, CQ = R // NX, KVW // NY
Y_ORDER = (4, 3, 5, 2, 6, 1, 7, 0)
KB = 256
STEPS = D // KB
LAG = 4
CHUNKS = 8
CW = D // CHUNKS


def kernel(seeds, plan, x_hbm, kv_hbm, br_hbm, cmp_out, sg_out,
           xo, xp, kvo, kvp, kvg, proj, btab, ctab, acc_o, acc_p, side, tf, tb, xr, qs, qown, yr, zb, fin,
           br, rc, sgs,
           loc_sem, in_send, in_recv, xs_sem, xr_sem, ys_sem, yr_sem, zs_sem, zr_sem,
           gys_sem, gyr_sem, gxs_sem, gxr_sem, ps_sem, pr_sem, cs_sem, cr_sem):
    me = lax.axis_index("dp")
    sec = lax.axis_index("pipe")
    core = me % 2
    y = (me // 2) % NY
    z = (me // (2 * NY)) % NZ
    x = me // (2 * NY * NZ)

    def dp(xx, zz, yy, cc):
        return ((xx * NZ + zz) * NY + yy) * 2 + cc

    partner = (dp(x, z, y, 1 - core), sec)
    x_peer = [(dp((x + d) % NX, z, y, core), sec) for d in range(1, NX)]
    y_peer = [(dp(x, z, (y + off) % NY, core), sec) for off in Y_ORDER[:-1]]
    z_peer = [(dp(x, (z + d) % NZ, y, core), sec) for d in range(1, NZ)]
    below = (me, (sec + SECTIONS - 1) % SECTIONS)
    above = (me, (sec + 1) % SECTIONS)
    peers = [partner, *x_peer, *y_peer, *z_peer, below, above]

    def remote(src, dst, send, recv, device):
        return pltpu.make_async_remote_copy(
            src_ref=src, dst_ref=dst, send_sem=send, recv_sem=recv, device_id=device, device_id_type=MESH
        )

    barrier = pltpu.get_barrier_semaphore()
    for device in peers:
        pl.semaphore_signal(barrier, inc=1, device_id=device, device_id_type=MESH)
    own_cols = pl.ds(pl.multiple_of(core * KVW, KVW), KVW)
    other_cols = pl.ds(pl.multiple_of((1 - core) * KVW, KVW), KVW)
    get_br = pltpu.make_async_copy(br_hbm, br, loc_sem.at[0])
    get_x = pltpu.make_async_copy(x_hbm, xo, loc_sem.at[1])
    get_kv = pltpu.make_async_copy(kv_hbm.at[:, :, own_cols], kvo, loc_sem.at[2])
    get_br.start()
    get_x.start()
    get_kv.start()

    seed = seeds[0, core]
    inv = jnp.float32(1.0 / MOD)
    scale = math.sqrt(3.0 / D)
    slope = jnp.float32(2.0 / 32748.0 * scale)
    low = jnp.float32(-scale)
    high = jnp.float32((2.0 * MOD / 32748.0 - 1.0) * scale)

    def centred(value):
        rest = value - (value.astype(jnp.float32) * inv + 0.5).astype(jnp.int32) * MOD
        return rest

    col = lax.broadcasted_iota(jnp.int32, (R, 128), 0)
    btab[...] = centred(col * 2053)
    ctab[...] = col * 29 + seed

    def make(step):
        for half in range(KB // 128):
            base = pl.multiple_of(step * KB, KB) + half * 128
            row = lax.broadcasted_iota(jnp.int32, (1, 128), 1) + base
            a = centred(row * 1031 + (seed * 3 + 7))
            e = row * 17 + 5
            for g in range(R // 64):
                rows = slice(g * 64, g * 64 + 64)
                one = btab[rows, :] + a
                two = one * one + e
                two = two - (two.astype(jnp.float32) * inv).astype(jnp.int32) * MOD
                three = two * two + ctab[rows, :]
                three = three - (three.astype(jnp.float32) * inv + 0.5).astype(jnp.int32) * MOD
                value = three.astype(jnp.float32) * slope + jnp.where(three < 0, high, low)
                proj[rows, pl.ds(base, 128)] = value.astype(jnp.bfloat16)

    def multiply(step, inputs, acc):
        cols = pl.ds(pl.multiple_of(step * KB, KB), KB)
        acc[...] += lax.dot_general(
            proj[:, cols], inputs[:, cols], (((1,), (1,)), ((), ())), preferred_element_type=jnp.float32
        )

    acc_o[...] = jnp.zeros_like(acc_o)
    acc_p[...] = jnp.zeros_like(acc_p)

    @pl.loop(0, LAG)
    def _(step):
        make(step)

    pl.semaphore_wait(barrier, len(peers))
    halves = [pl.ds(h * (D // 2), D // 2) for h in range(2)]
    give = [remote(x_hbm.at[:, halves[h]], xp.at[:, halves[h]], in_send.at[h], in_recv.at[h], partner) for h in range(2)]
    give.append(remote(kv_hbm.at[:, :, other_cols], kvp, in_send.at[2], in_recv.at[2], partner))
    for copy in give:
        copy.start()
    get_br.wait()

    def chunk(k):
        return pl.ds(pl.multiple_of(k * CW, CW), CW)

    def relay(source, k):
        return remote(source.at[:, chunk(k)], rc.at[:, chunk(k)], cs_sem.at[k], cr_sem.at[k], below)

    @pl.when(sec == SECTIONS - 1)
    def _():
        for k in range(CHUNKS):
            relay(br, k).start()
        sg_out[...] = br[...]

    def chain(point):
        k = point - 2 * (SECTIONS - 2 - sec)

        @pl.when((sec < SECTIONS - 1) & (k >= 0) & (k < CHUNKS))
        def _():
            relay(br, k).wait_recv()
            cols = chunk(k)
            total = (rc[:, cols].astype(jnp.float32) + br[:, cols].astype(jnp.float32)).astype(jnp.bfloat16)
            sgs[:, cols] = total
            sg_out[:, cols] = total

            @pl.when(sec > 0)
            def _():
                relay(sgs, k).start()

    get_x.wait()

    @pl.loop(LAG, STEPS // 2)
    def _(step):
        make(step)
        multiply(step - LAG, xo, acc_o)

    give[0].wait_recv()

    @pl.loop(STEPS // 2, STEPS)
    def _(step):
        make(step)
        multiply(step - LAG, xo, acc_o)
        multiply(step - STEPS // 2, xp, acc_p)

    @pl.loop(STEPS - LAG, STEPS)
    def _(step):
        multiply(step, xo, acc_o)

    give[1].wait_recv()

    @pl.loop(STEPS // 2, STEPS)
    def _(step):
        multiply(step, xp, acc_p)

    side[:, :ROWS] = acc_o[...].astype(jnp.bfloat16)
    side[:, ROWS:] = acc_p[...].astype(jnp.bfloat16)
    get_kv.wait()
    give[2].wait_recv()
    for slot in range(MBW):
        batch = plan[0, slot]
        kvg[slot * TOK:(slot + 1) * TOK, :] = kvo[batch]
        kvg[ROWS + slot * TOK:ROWS + (slot + 1) * TOK, :] = kvp[batch]
    chain(0)

    copies = []

    def start(copy):
        copy.start()
        copies.append(copy)
        return copy

    blocks = [(y + off) % NY for off in Y_ORDER]
    x_copy = {}

    def send_x(j):
        for d in range(1, NX):
            x_copy[d, j] = start(
                remote(tb.at[(x + d) % NX, j], xr.at[d - 1, j], xs_sem.at[d - 1, j], xr_sem.at[d - 1, j], x_peer[d - 1])
            )

    for j in range(NY):
        cols = pl.ds(pl.multiple_of(blocks[j] * CQ, CQ), CQ)
        part = jnp.dot(side[...], kvg[:, cols], preferred_element_type=jnp.float32)
        for q in range(NX):
            piece = part[q * RQ:(q + 1) * RQ, :]
            tf[q, j] = piece
            tb[q, j] = piece.astype(jnp.bfloat16)
        if j:
            send_x(j - 1)
    send_x(NY - 1)
    chain(1)

    y_copy = []
    for j in range(NY):
        total = tf[x, j]
        for d in range(1, NX):
            x_copy[d, j].wait_recv()
            total = total + xr[d - 1, j].astype(jnp.float32)
        if j < NY - 1:
            qs[j] = total.astype(jnp.bfloat16)
            y_copy.append(start(remote(qs.at[j], yr.at[j], ys_sem.at[j], yr_sem.at[j], y_peer[j])))
        else:
            qown[...] = total
        if j in (1, 4):
            chain(2 if j == 1 else 3)

    chain(4)
    total = qown[...]
    for j in range(NY - 1):
        y_copy[j].wait_recv()
        total = total + yr[j].astype(jnp.float32)
    zb[z] = total.astype(jnp.bfloat16)
    z_copy = [
        start(remote(zb.at[z], zb.at[z], zs_sem.at[d], zr_sem.at[d], z_peer[d])) for d in range(NZ - 1)
    ]
    chain(5)
    for copy in z_copy:
        copy.wait_recv()
    total = (zb[0].astype(jnp.float32) + zb[1].astype(jnp.float32)) + zb[2].astype(jnp.float32)
    fin[core, x, y] = total.astype(jnp.bfloat16)

    mine = fin.at[core, x, y]
    gy_copy = [start(remote(mine, mine, gys_sem.at[j], gyr_sem.at[j], y_peer[j])) for j in range(NY - 1)]
    gx_copy = {}

    def to_partner(xx, yy):
        piece = fin.at[core, xx, yy]
        remote(piece, piece, ps_sem, pr_sem, partner).start()

    for j in range(NY - 1, -1, -1):
        yy = (y - Y_ORDER[j]) % NY
        if j < NY - 1:
            gy_copy[j].wait_recv()
        piece = fin.at[core, x, yy]
        for d in range(1, NX):
            gx_copy[d, j] = start(remote(piece, piece, gxs_sem.at[d - 1, j], gxr_sem.at[d - 1, j], x_peer[d - 1]))
        to_partner(x, yy)
        if j in (6, 3):
            chain(6 if j == 6 else 7)
    chain(8)
    for j in range(NY - 1, -1, -1):
        yy = (y - Y_ORDER[j]) % NY
        for d in range(1, NX):
            gx_copy[d, j].wait_recv()
            to_partner((x + NX - d) % NX, yy)
        if j in (5, 2):
            chain(9 if j == 5 else 10)
    chain(11)
    whole = remote(fin.at[core], fin.at[core], ps_sem, pr_sem, partner)
    whole.wait_recv()
    for role in range(2):
        for q in range(NX):
            for b in range(NY):
                cmp_out[q * RQ:(q + 1) * RQ, role * KVW + b * CQ:role * KVW + (b + 1) * CQ] = fin[role, q, b]
    whole.wait_send()
    for copy in copies + give:
        copy.wait_send()

    @pl.when(sec > 0)
    def _():
        for k in range(CHUNKS):
            relay(br, k).wait_send()


def per_device(stashed, kv_grads, branch_grads, flora_seeds, plan):
    vmem = pltpu.VMEM
    bf16, f32, i32 = jnp.bfloat16, jnp.float32, jnp.int32
    dma = pltpu.SemaphoreType.DMA
    compressed, grads = pl.pallas_call(
        kernel,
        out_shape=(jax.ShapeDtypeStruct((R, 2 * KVW), bf16), jax.ShapeDtypeStruct((TOK, D), bf16)),
        in_specs=[pl.BlockSpec(memory_space=pltpu.SMEM)] * 2 + [pl.BlockSpec(memory_space=pl.ANY)] * 3,
        out_specs=(pl.BlockSpec(memory_space=vmem), pl.BlockSpec(memory_space=vmem)),
        scratch_shapes=[
            vmem((ROWS, D), bf16), vmem((ROWS, D), bf16),
            vmem((MBW, TOK, KVW), bf16), vmem((MBW, TOK, KVW), bf16), vmem((2 * ROWS, KVW), bf16),
            vmem((R, D), bf16), vmem((R, 128), i32), vmem((R, 128), i32),
            vmem((R, ROWS), f32), vmem((R, ROWS), f32), vmem((R, 2 * ROWS), bf16),
            vmem((NX, NY, RQ, CQ), f32), vmem((NX, NY, RQ, CQ), bf16), vmem((NX - 1, NY, RQ, CQ), bf16),
            vmem((NY - 1, RQ, CQ), bf16), vmem((RQ, CQ), f32), vmem((NY - 1, RQ, CQ), bf16),
            vmem((NZ, RQ, CQ), bf16), vmem((2, NX, NY, RQ, CQ), bf16),
            vmem((TOK, D), bf16), vmem((TOK, D), bf16), vmem((TOK, D), bf16),
            dma((3,)), dma((3,)), dma((3,)),
            dma((NX - 1, NY)), dma((NX - 1, NY)), dma((NY - 1,)), dma((NY - 1,)), dma((NZ - 1,)), dma((NZ - 1,)),
            dma((NY - 1,)), dma((NY - 1,)), dma((NX - 1, NY)), dma((NX - 1, NY)), dma, dma,
            dma((CHUNKS,)), dma((CHUNKS,)),
        ],
        compiler_params=pltpu.CompilerParams(
            collective_id=0, has_side_effects=True, vmem_limit_bytes=60 * 1024 * 1024
        ),
    )(flora_seeds, plan, stashed.reshape(ROWS, D), kv_grads.reshape(MBW, TOK, 2 * KVW), branch_grads.reshape(TOK, D))
    return compressed.astype(f32)[None], grads[None]


def solution(mesh):
    placed = (
        P("pipe", None, "dp", None),
        P("pipe", None, "dp", None),
        P("pipe", "dp", None),
        P("pipe", None),
        P("pipe", None),
    )
    return jax.shard_map(
        per_device,
        mesh=mesh,
        in_specs=placed,
        out_specs=(P("pipe", None, None), P("pipe", "dp", None)),
        check_vma=False,
    )
```

```python
import math

import jax
import jax.numpy as jnp
from jax import lax
from jax.experimental import pallas as pl
from jax.experimental.pallas import tpu as pltpu
from jax.sharding import PartitionSpec as P

MESH = pl.DeviceIdType.MESH
NX, NZ, NY, SECTIONS = 4, 3, 8, 4
R, D, KVW, MBW, TOK = 256, 8192, 1024, 4, 32
ROWS = MBW * TOK
MOD = 32749
RQ, CQ = R // NX, KVW // NY
Y_ORDER = (4, 3, 5, 2, 6, 1, 7, 0)
KB = 512
STEPS = D // KB
LAG = 2
TAIL = 1024
CHUNKS = 16
CW = D // CHUNKS
WINDOW = 4


def kernel(seeds, plan, x_hbm, kv_hbm, br_hbm, cmp_out, sg_out,
           xo, xp, kvo, kvp, kvg, proj, btab, ctab, acc_o, acc_p, side, tf, tb, xr, qs, qown, yr, zb, fin,
           br, rc, sgs, above_sum, br_sem, rs_sem, rr_sem,
           loc_sem, in_send, in_recv, xs_sem, xr_sem, ys_sem, yr_sem, zs_sem, zr_sem,
           gys_sem, gyr_sem, gxs_sem, gxr_sem, ps_sem, pr_sem, cs_sem, cr_sem):
    me = lax.axis_index("dp")
    sec = lax.axis_index("pipe")
    core = me % 2
    y = (me // 2) % NY
    z = (me // (2 * NY)) % NZ
    x = me // (2 * NY * NZ)

    def dp(xx, zz, yy, cc):
        return ((xx * NZ + zz) * NY + yy) * 2 + cc

    partner = (dp(x, z, y, 1 - core), sec)
    x_peer = [(dp((x + d) % NX, z, y, core), sec) for d in range(1, NX)]
    y_peer = [(dp(x, z, (y + off) % NY, core), sec) for off in Y_ORDER[:-1]]
    z_peer = [(dp(x, (z + d) % NZ, y, core), sec) for d in range(1, NZ)]
    below = (me, (sec + SECTIONS - 1) % SECTIONS)
    above = (me, (sec + 1) % SECTIONS)
    peers = [partner, *x_peer, *y_peer, *z_peer, below, above]

    def remote(src, dst, send, recv, device):
        return pltpu.make_async_remote_copy(
            src_ref=src, dst_ref=dst, send_sem=send, recv_sem=recv, device_id=device, device_id_type=MESH
        )

    barrier = pltpu.get_barrier_semaphore()
    for device in peers:
        pl.semaphore_signal(barrier, inc=1, device_id=device, device_id_type=MESH)

    own_cols = pl.ds(pl.multiple_of(core * KVW, KVW), KVW)
    other_cols = pl.ds(pl.multiple_of((1 - core) * KVW, KVW), KVW)
    get_br = [
        pltpu.make_async_copy(br_hbm.at[:, k * CW:(k + 1) * CW], br.at[k], br_sem.at[k]) for k in range(CHUNKS)
    ]
    get_x = pltpu.make_async_copy(x_hbm, xo, loc_sem.at[1])
    get_kv = pltpu.make_async_copy(kv_hbm.at[:, :, own_cols], kvo, loc_sem.at[2])
    for copy in get_br:
        copy.start()
    get_x.start()
    get_kv.start()

    seed = seeds[0, core]
    inv = jnp.float32(1.0 / MOD)
    scale = math.sqrt(3.0 / D)
    slope = jnp.float32(2.0 / 32748.0 * scale)
    low = jnp.float32(-scale)
    inv_up = jnp.float32((1.0 + 5e-7) / MOD)

    def centred(value):
        rest = value - (value.astype(jnp.float32) * inv + 0.5).astype(jnp.int32) * MOD
        return rest

    col = lax.broadcasted_iota(jnp.int32, (R, 128), 0)
    btab[...] = centred(col * 2053)
    ctab[...] = col * 29 + seed

    def make(step):
        for half in range(KB // 128):
            base = pl.multiple_of(step * KB, KB) + half * 128
            row = lax.broadcasted_iota(jnp.int32, (1, 128), 1) + base
            a = centred(row * 1031 + (seed * 3 + 7))
            e = row * 17 + 5
            for g in range(R // 64):
                rows = slice(g * 64, g * 64 + 64)
                one = btab[rows, :] + a
                two = one * one + e
                two = two - (two.astype(jnp.float32) * inv).astype(jnp.int32) * MOD
                three = two * two + ctab[rows, :]
                rest = (three - (three >> 15) * MOD).astype(jnp.float32)
                rest = rest - jnp.floor(rest * inv_up) * jnp.float32(MOD)
                value = rest * slope + low
                proj[rows, pl.ds(base, 128)] = value.astype(jnp.bfloat16)

    def multiply(step, width, inputs, acc):
        cols = pl.ds(pl.multiple_of(step * width, width), width)
        acc[...] += lax.dot_general(
            proj[:, cols], inputs[:, cols], (((1,), (1,)), ((), ())), preferred_element_type=jnp.float32
        )

    acc_o[...] = jnp.zeros_like(acc_o)
    acc_p[...] = jnp.zeros_like(acc_p)

    @pl.loop(0, LAG)
    def _(step):
        make(step)

    pl.semaphore_wait(barrier, len(peers))
    halves = [pl.ds(h * (D // 2), D // 2) for h in range(2)]
    give = [remote(x_hbm.at[:, halves[h]], xp.at[:, halves[h]], in_send.at[h], in_recv.at[h], partner) for h in range(2)]
    give.append(remote(kv_hbm.at[:, :, other_cols], kvp, in_send.at[2], in_recv.at[2], partner))
    for copy in give:
        copy.start()
    for copy in get_br:
        copy.wait()

    def raw(k):
        return remote(br.at[k], rc.at[k], cs_sem.at[k], cr_sem.at[k], (me, sec + 1 - 2 * (sec % 2)))

    def relay(k):
        return remote(sgs.at[k], above_sum.at[k], rs_sem.at[k], rr_sem.at[k], (me, SECTIONS - 1 - sec))

    def added(first, second):
        return (first.astype(jnp.float32) + second.astype(jnp.float32)).astype(jnp.bfloat16)

    @pl.when(sec >= 2)
    def _():
        for k in range(WINDOW):
            raw(k).start()

    @pl.when(sec == 1)
    def _():
        for k in range(CHUNKS):
            raw(k).start()

    @pl.when(sec == SECTIONS - 1)
    def _():
        for k in range(CHUNKS):
            sg_out[:, k * CW:(k + 1) * CW] = br[k]

    def chain(k):
        @pl.when(sec >= 2)
        def _():
            raw(k).wait_recv()
            total = added(rc[k], br[k])
            sgs[k] = total

            @pl.when(sec == 2)
            def _():
                sg_out[:, k * CW:(k + 1) * CW] = total

            if k + WINDOW < CHUNKS:
                raw(k + WINDOW).start()
            relay(k).start()

    get_x.wait()

    @pl.loop(LAG, STEPS)
    def _(step):
        make(step)
        multiply(step - LAG, KB, xo, acc_o)

    chain(0)
    multiply(D // TAIL - 1, TAIL, xo, acc_o)
    for copy in give[:2]:
        copy.wait_recv()

    @pl.loop(0, D // TAIL)
    def _(step):
        multiply(step, TAIL, xp, acc_p)

    chain(1)
    side[:, :ROWS] = acc_o[...].astype(jnp.bfloat16)
    side[:, ROWS:] = acc_p[...].astype(jnp.bfloat16)
    get_kv.wait()
    give[2].wait_recv()
    for slot in range(MBW):
        batch = plan[0, slot]
        kvg[slot * TOK:(slot + 1) * TOK, :] = kvo[batch]
        kvg[ROWS + slot * TOK:ROWS + (slot + 1) * TOK, :] = kvp[batch]

    copies = []

    def start(copy):
        copy.start()
        copies.append(copy)
        return copy

    blocks = [(y + off) % NY for off in Y_ORDER]
    x_copy = {}

    def send_x(j):
        for d in range(1, NX):
            x_copy[d, j] = start(
                remote(tb.at[(x + d) % NX, j], xr.at[d - 1, j], xs_sem.at[d - 1, j], xr_sem.at[d - 1, j], x_peer[d - 1])
            )

    for j in range(NY):
        cols = pl.ds(pl.multiple_of(blocks[j] * CQ, CQ), CQ)
        part = jnp.dot(side[...], kvg[:, cols], preferred_element_type=jnp.float32)
        for q in range(NX):
            piece = part[q * RQ:(q + 1) * RQ, :]
            tf[q, j] = piece
            tb[q, j] = piece.astype(jnp.bfloat16)
        if j:
            send_x(j - 1)
    send_x(NY - 1)
    chain(2)

    y_copy = []
    for j in range(NY):
        total = tf[x, j]
        for d in range(1, NX):
            x_copy[d, j].wait_recv()
            total = total + xr[d - 1, j].astype(jnp.float32)
        if j < NY - 1:
            qs[j] = total.astype(jnp.bfloat16)
            y_copy.append(start(remote(qs.at[j], yr.at[j], ys_sem.at[j], yr_sem.at[j], y_peer[j])))
        else:
            qown[...] = total
        if j % 2:
            chain(3 + j // 2)

    total = qown[...]
    for j in range(NY - 1):
        y_copy[j].wait_recv()
        total = total + yr[j].astype(jnp.float32)
        if j in (2, 5):
            chain(7 + j // 3)
    zb[z] = total.astype(jnp.bfloat16)
    z_copy = [
        start(remote(zb.at[z], zb.at[z], zs_sem.at[d], zr_sem.at[d], z_peer[d])) for d in range(NZ - 1)
    ]
    chain(9)
    for copy in z_copy:
        copy.wait_recv()
    total = (zb[0].astype(jnp.float32) + zb[1].astype(jnp.float32)) + zb[2].astype(jnp.float32)
    fin[core, x, y] = total.astype(jnp.bfloat16)

    mine = fin.at[core, x, y]
    gy_copy = [start(remote(mine, mine, gys_sem.at[j], gyr_sem.at[j], y_peer[j])) for j in range(NY - 1)]
    gx_copy = {}

    def to_partner(xx, yy):
        piece = fin.at[core, xx, yy]
        remote(piece, piece, ps_sem, pr_sem, partner).start()

    for j in range(NY - 1, -1, -1):
        yy = (y - Y_ORDER[j]) % NY
        if j < NY - 1:
            gy_copy[j].wait_recv()
        piece = fin.at[core, x, yy]
        for d in range(1, NX):
            gx_copy[d, j] = start(remote(piece, piece, gxs_sem.at[d - 1, j], gxr_sem.at[d - 1, j], x_peer[d - 1]))
        to_partner(x, yy)
        if j in (5, 3, 1):
            chain(10 + (5 - j) // 2)
    chain(13)
    for j in range(NY - 1, -1, -1):
        yy = (y - Y_ORDER[j]) % NY
        for d in range(1, NX):
            gx_copy[d, j].wait_recv()
            to_partner((x + NX - d) % NX, yy)
        if j in (5, 3):
            chain(14 + (5 - j) // 2)

    @pl.when(sec < 2)
    def _():
        @pl.loop(0, CHUNKS)
        def _(k):
            cols = pl.ds(pl.multiple_of(k * CW, CW), CW)
            relay(k).wait_recv()

            @pl.when(sec == 1)
            def _():
                sg_out[:, cols] = added(above_sum[k], br[k])

            @pl.when(sec == 0)
            def _():
                raw(k).wait_recv()
                sg_out[:, cols] = added(added(above_sum[k], rc[k]), br[k])

    whole = remote(fin.at[core], fin.at[core], ps_sem, pr_sem, partner)
    whole.wait_recv()
    for role in range(2):
        for q in range(NX):
            for b in range(NY):
                cmp_out[q * RQ:(q + 1) * RQ, role * KVW + b * CQ:role * KVW + (b + 1) * CQ] = fin[role, q, b]
    whole.wait_send()
    for copy in copies + give:
        copy.wait_send()

    @pl.when(sec > 0)
    def _():
        for k in range(CHUNKS):
            raw(k).wait_send()

    @pl.when(sec >= 2)
    def _():
        for k in range(CHUNKS):
            relay(k).wait_send()


def per_device(stashed, kv_grads, branch_grads, flora_seeds, plan):
    vmem = pltpu.VMEM
    bf16, f32, i32 = jnp.bfloat16, jnp.float32, jnp.int32
    dma = pltpu.SemaphoreType.DMA
    compressed, grads = pl.pallas_call(
        kernel,
        out_shape=(jax.ShapeDtypeStruct((R, 2 * KVW), bf16), jax.ShapeDtypeStruct((TOK, D), bf16)),
        in_specs=[pl.BlockSpec(memory_space=pltpu.SMEM)] * 2 + [pl.BlockSpec(memory_space=pl.ANY)] * 3,
        out_specs=(pl.BlockSpec(memory_space=vmem), pl.BlockSpec(memory_space=vmem)),
        scratch_shapes=[
            vmem((ROWS, D), bf16), vmem((ROWS, D), bf16),
            vmem((MBW, TOK, KVW), bf16), vmem((MBW, TOK, KVW), bf16), vmem((2 * ROWS, KVW), bf16),
            vmem((R, D), bf16), vmem((R, 128), i32), vmem((R, 128), i32),
            vmem((R, ROWS), f32), vmem((R, ROWS), f32), vmem((R, 2 * ROWS), bf16),
            vmem((NX, NY, RQ, CQ), f32), vmem((NX, NY, RQ, CQ), bf16), vmem((NX - 1, NY, RQ, CQ), bf16),
            vmem((NY - 1, RQ, CQ), bf16), vmem((RQ, CQ), f32), vmem((NY - 1, RQ, CQ), bf16),
            vmem((NZ, RQ, CQ), bf16), vmem((2, NX, NY, RQ, CQ), bf16),
            vmem((CHUNKS, TOK, CW), bf16), vmem((CHUNKS, TOK, CW), bf16), vmem((CHUNKS, TOK, CW), bf16),
            vmem((CHUNKS, TOK, CW), bf16), dma((CHUNKS,)), dma((CHUNKS,)), dma((CHUNKS,)),
            dma((3,)), dma((3,)), dma((3,)),
            dma((NX - 1, NY)), dma((NX - 1, NY)), dma((NY - 1,)), dma((NY - 1,)), dma((NZ - 1,)), dma((NZ - 1,)),
            dma((NY - 1,)), dma((NY - 1,)), dma((NX - 1, NY)), dma((NX - 1, NY)), dma, dma,
            dma((CHUNKS,)), dma((CHUNKS,)),
        ],
        compiler_params=pltpu.CompilerParams(
            collective_id=0, has_side_effects=True, vmem_limit_bytes=60 * 1024 * 1024
        ),
    )(flora_seeds, plan, stashed.reshape(ROWS, D), kv_grads.reshape(MBW, TOK, 2 * KVW), branch_grads.reshape(TOK, D))
    return compressed.astype(f32)[None], grads[None]


def solution(mesh):
    placed = (
        P("pipe", None, "dp", None),
        P("pipe", None, "dp", None),
        P("pipe", "dp", None),
        P("pipe", None),
        P("pipe", None),
    )
    return jax.shard_map(
        per_device,
        mesh=mesh,
        in_specs=placed,
        out_specs=(P("pipe", None, None), P("pipe", "dp", None)),
        check_vma=False,
    )
```

```python
import math

import jax
import jax.numpy as jnp
from jax import lax
from jax.experimental import pallas as pl
from jax.experimental.pallas import tpu as pltpu
from jax.sharding import PartitionSpec as P

MESH = pl.DeviceIdType.MESH
NX, NZ, NY, SECTIONS = 4, 3, 8, 4
R, D, KVW, MBW, TOK = 256, 8192, 1024, 4, 32
ROWS = MBW * TOK
MOD = 32749
RQ, CQ = R // NX, KVW // NY
Y_ORDER = (4, 3, 5, 2, 6, 1, 7, 0)
KB = 512
STEPS = D // KB
LAG = 2
TAIL = 1024
CHUNKS = 16
CW = D // CHUNKS
AHEAD = 4
WINDOW = 4


def kernel(seeds, plan, x_hbm, kv_hbm, br_hbm, cmp_out, sg_out,
           xo, xp, kvo, kvp, kvg, proj, btab, ctab, acc_o, acc_p, side, tf, tb, xr, qs, qown, yr, zb, fin,
           br, rc, sgs, above_sum, br_sem, rs_sem, rr_sem,
           loc_sem, in_send, in_recv, xs_sem, xr_sem, ys_sem, yr_sem, zs_sem, zr_sem,
           gys_sem, gyr_sem, gxs_sem, gxr_sem, ps_sem, pr_sem, cs_sem, cr_sem):
    me = lax.axis_index("dp")
    sec = lax.axis_index("pipe")
    core = me % 2
    y = (me // 2) % NY
    z = (me // (2 * NY)) % NZ
    x = me // (2 * NY * NZ)

    def dp(xx, zz, yy, cc):
        return ((xx * NZ + zz) * NY + yy) * 2 + cc

    partner = (dp(x, z, y, 1 - core), sec)
    x_peer = [(dp((x + d) % NX, z, y, core), sec) for d in range(1, NX)]
    y_peer = [(dp(x, z, (y + off) % NY, core), sec) for off in Y_ORDER[:-1]]
    z_peer = [(dp(x, (z + d) % NZ, y, core), sec) for d in range(1, NZ)]
    below = (me, (sec + SECTIONS - 1) % SECTIONS)
    above = (me, (sec + 1) % SECTIONS)
    peers = [partner, *x_peer, *y_peer, *z_peer, below, above]

    def remote(src, dst, send, recv, device):
        return pltpu.make_async_remote_copy(
            src_ref=src, dst_ref=dst, send_sem=send, recv_sem=recv, device_id=device, device_id_type=MESH
        )

    barrier = pltpu.get_barrier_semaphore()
    for device in peers:
        pl.semaphore_signal(barrier, inc=1, device_id=device, device_id_type=MESH)

    own_cols = pl.ds(pl.multiple_of(core * KVW, KVW), KVW)
    other_cols = pl.ds(pl.multiple_of((1 - core) * KVW, KVW), KVW)
    get_br = [
        pltpu.make_async_copy(br_hbm.at[:, k * CW:(k + 1) * CW], br.at[k], br_sem.at[k]) for k in range(CHUNKS)
    ]
    get_x = pltpu.make_async_copy(x_hbm, xo, loc_sem.at[1])
    get_kv = pltpu.make_async_copy(kv_hbm.at[:, :, own_cols], kvo, loc_sem.at[2])
    for copy in get_br:
        copy.start()
    get_x.start()
    get_kv.start()

    seed = seeds[0, core]
    inv = jnp.float32(1.0 / MOD)
    scale = math.sqrt(3.0 / D)
    slope = jnp.float32(2.0 / 32748.0 * scale)
    low = jnp.float32(-scale)
    inv_up = jnp.float32((1.0 + 5e-7) / MOD)

    def centred(value):
        rest = value - (value.astype(jnp.float32) * inv + 0.5).astype(jnp.int32) * MOD
        return rest

    col = lax.broadcasted_iota(jnp.int32, (R, 128), 0)
    btab[...] = centred(col * 2053)
    ctab[...] = col * 29 + seed

    def make(step):
        for half in range(KB // 128):
            base = pl.multiple_of(step * KB, KB) + half * 128
            row = lax.broadcasted_iota(jnp.int32, (1, 128), 1) + base
            a = centred(row * 1031 + (seed * 3 + 7))
            e = row * 17 + 5
            for g in range(R // 64):
                rows = slice(g * 64, g * 64 + 64)
                one = btab[rows, :] + a
                two = one * one + e
                two = two - (two.astype(jnp.float32) * inv).astype(jnp.int32) * MOD
                three = two * two + ctab[rows, :]
                rest = (three - (three >> 15) * MOD).astype(jnp.float32)
                rest = rest - jnp.floor(rest * inv_up) * jnp.float32(MOD)
                value = rest * slope + low
                proj[rows, pl.ds(base, 128)] = value.astype(jnp.bfloat16)

    def multiply(step, width, inputs, acc):
        cols = pl.ds(pl.multiple_of(step * width, width), width)
        acc[...] += lax.dot_general(
            proj[:, cols], inputs[:, cols], (((1,), (1,)), ((), ())), preferred_element_type=jnp.float32
        )

    acc_o[...] = jnp.zeros_like(acc_o)
    acc_p[...] = jnp.zeros_like(acc_p)

    @pl.loop(0, LAG)
    def _(step):
        make(step)

    pl.semaphore_wait(barrier, len(peers))
    halves = [pl.ds(h * (D // 2), D // 2) for h in range(2)]
    give = [remote(x_hbm.at[:, halves[h]], xp.at[:, halves[h]], in_send.at[h], in_recv.at[h], partner) for h in range(2)]
    give.append(remote(kv_hbm.at[:, :, other_cols], kvp, in_send.at[2], in_recv.at[2], partner))
    for copy in give:
        copy.start()
    for copy in get_br:
        copy.wait()

    def raw(k):
        return remote(br.at[k], rc.at[k], cs_sem.at[k], cr_sem.at[k], (me, sec + 1 - 2 * (sec % 2)))

    def relay(k):
        return remote(sgs.at[k], above_sum.at[k], rs_sem.at[k], rr_sem.at[k], (me, SECTIONS - 1 - sec))

    def added(first, second):
        return (first.astype(jnp.float32) + second.astype(jnp.float32)).astype(jnp.bfloat16)

    @pl.when(sec >= 2)
    def _():
        for k in range(WINDOW):
            raw(k).start()

    @pl.when(sec == 1)
    def _():
        raw(0).start()

    @pl.when(sec == SECTIONS - 1)
    def _():
        for k in range(CHUNKS):
            sg_out[:, k * CW:(k + 1) * CW] = br[k]

    def chain(k):
        if k + 1 < CHUNKS:
            @pl.when(sec == 1)
            def _():
                raw(k + 1).start()

        @pl.when(sec >= 2)
        def _():
            raw(k).wait_recv()
            total = added(rc[k], br[k])
            sgs[k] = total

            @pl.when(sec == 2)
            def _():
                sg_out[:, k * CW:(k + 1) * CW] = total

            if k + WINDOW < CHUNKS:
                raw(k + WINDOW).start()
            relay(k).start()

    get_x.wait()

    @pl.loop(LAG, STEPS)
    def _(step):
        make(step)
        multiply(step - LAG, KB, xo, acc_o)

    chain(0)
    multiply(D // TAIL - 1, TAIL, xo, acc_o)
    for copy in give[:2]:
        copy.wait_recv()

    @pl.loop(0, D // TAIL)
    def _(step):
        multiply(step, TAIL, xp, acc_p)

    chain(1)
    side[:, :ROWS] = acc_o[...].astype(jnp.bfloat16)
    side[:, ROWS:] = acc_p[...].astype(jnp.bfloat16)
    get_kv.wait()
    give[2].wait_recv()
    for slot in range(MBW):
        batch = plan[0, slot]
        kvg[slot * TOK:(slot + 1) * TOK, :] = kvo[batch]
        kvg[ROWS + slot * TOK:ROWS + (slot + 1) * TOK, :] = kvp[batch]

    copies = []

    def start(copy):
        copy.start()
        copies.append(copy)
        return copy

    blocks = [(y + off) % NY for off in Y_ORDER]
    x_copy = {}

    def send_x(j):
        for d in range(1, NX):
            x_copy[d, j] = start(
                remote(tb.at[(x + d) % NX, j], xr.at[d - 1, j], xs_sem.at[d - 1, j], xr_sem.at[d - 1, j], x_peer[d - 1])
            )

    for j in range(NY):
        cols = pl.ds(pl.multiple_of(blocks[j] * CQ, CQ), CQ)
        part = jnp.dot(side[...], kvg[:, cols], preferred_element_type=jnp.float32)
        for q in range(NX):
            piece = part[q * RQ:(q + 1) * RQ, :]
            tf[q, j] = piece
            tb[q, j] = piece.astype(jnp.bfloat16)
        if 0 < j <= AHEAD:
            send_x(j - 1)
    chain(2)

    y_copy = []
    for j in range(NY):
        total = tf[x, j]
        for d in range(1, NX):
            x_copy[d, j].wait_recv()
            total = total + xr[d - 1, j].astype(jnp.float32)
        if j + AHEAD < NY:
            send_x(j + AHEAD)
        if j < NY - 1:
            qs[j] = total.astype(jnp.bfloat16)
            y_copy.append(start(remote(qs.at[j], yr.at[j], ys_sem.at[j], yr_sem.at[j], y_peer[j])))
        else:
            qown[...] = total
        if j % 2:
            chain(3 + j // 2)

    total = qown[...]
    for j in range(NY - 1):
        y_copy[j].wait_recv()
        total = total + yr[j].astype(jnp.float32)
        if j in (2, 5):
            chain(7 + j // 3)
    zb[z] = total.astype(jnp.bfloat16)
    z_copy = [
        start(remote(zb.at[z], zb.at[z], zs_sem.at[d], zr_sem.at[d], z_peer[d])) for d in range(NZ - 1)
    ]
    chain(9)
    for copy in z_copy:
        copy.wait_recv()
    total = (zb[0].astype(jnp.float32) + zb[1].astype(jnp.float32)) + zb[2].astype(jnp.float32)
    fin[core, x, y] = total.astype(jnp.bfloat16)

    mine = fin.at[core, x, y]
    gy_copy = [start(remote(mine, mine, gys_sem.at[j], gyr_sem.at[j], y_peer[j])) for j in range(NY - 1)]
    gx_copy = {}

    def to_partner(xx, yy):
        piece = fin.at[core, xx, yy]
        remote(piece, piece, ps_sem, pr_sem, partner).start()

    for j in range(NY - 1, -1, -1):
        yy = (y - Y_ORDER[j]) % NY
        if j < NY - 1:
            gy_copy[j].wait_recv()
        piece = fin.at[core, x, yy]
        for d in range(1, NX):
            gx_copy[d, j] = start(remote(piece, piece, gxs_sem.at[d - 1, j], gxr_sem.at[d - 1, j], x_peer[d - 1]))
        to_partner(x, yy)
        if j in (5, 3, 1):
            chain(10 + (5 - j) // 2)
    chain(13)
    for j in range(NY - 1, -1, -1):
        yy = (y - Y_ORDER[j]) % NY
        for d in range(1, NX):
            gx_copy[d, j].wait_recv()
            to_partner((x + NX - d) % NX, yy)
        if j in (5, 3):
            chain(14 + (5 - j) // 2)

    @pl.when(sec < 2)
    def _():
        @pl.loop(0, CHUNKS)
        def _(k):
            cols = pl.ds(pl.multiple_of(k * CW, CW), CW)
            relay(k).wait_recv()

            @pl.when(sec == 1)
            def _():
                sg_out[:, cols] = added(above_sum[k], br[k])

            @pl.when(sec == 0)
            def _():
                raw(k).wait_recv()
                sg_out[:, cols] = added(added(above_sum[k], rc[k]), br[k])

    whole = remote(fin.at[core], fin.at[core], ps_sem, pr_sem, partner)
    whole.wait_recv()
    for role in range(2):
        for q in range(NX):
            for b in range(NY):
                cmp_out[q * RQ:(q + 1) * RQ, role * KVW + b * CQ:role * KVW + (b + 1) * CQ] = fin[role, q, b]
    whole.wait_send()
    for copy in copies + give:
        copy.wait_send()

    @pl.when(sec > 0)
    def _():
        for k in range(CHUNKS):
            raw(k).wait_send()

    @pl.when(sec >= 2)
    def _():
        for k in range(CHUNKS):
            relay(k).wait_send()


def per_device(stashed, kv_grads, branch_grads, flora_seeds, plan):
    vmem = pltpu.VMEM
    bf16, f32, i32 = jnp.bfloat16, jnp.float32, jnp.int32
    dma = pltpu.SemaphoreType.DMA
    compressed, grads = pl.pallas_call(
        kernel,
        out_shape=(jax.ShapeDtypeStruct((R, 2 * KVW), bf16), jax.ShapeDtypeStruct((TOK, D), bf16)),
        in_specs=[pl.BlockSpec(memory_space=pltpu.SMEM)] * 2 + [pl.BlockSpec(memory_space=pl.ANY)] * 3,
        out_specs=(pl.BlockSpec(memory_space=vmem), pl.BlockSpec(memory_space=vmem)),
        scratch_shapes=[
            vmem((ROWS, D), bf16), vmem((ROWS, D), bf16),
            vmem((MBW, TOK, KVW), bf16), vmem((MBW, TOK, KVW), bf16), vmem((2 * ROWS, KVW), bf16),
            vmem((R, D), bf16), vmem((R, 128), i32), vmem((R, 128), i32),
            vmem((R, ROWS), f32), vmem((R, ROWS), f32), vmem((R, 2 * ROWS), bf16),
            vmem((NX, NY, RQ, CQ), f32), vmem((NX, NY, RQ, CQ), bf16), vmem((NX - 1, NY, RQ, CQ), bf16),
            vmem((NY - 1, RQ, CQ), bf16), vmem((RQ, CQ), f32), vmem((NY - 1, RQ, CQ), bf16),
            vmem((NZ, RQ, CQ), bf16), vmem((2, NX, NY, RQ, CQ), bf16),
            vmem((CHUNKS, TOK, CW), bf16), vmem((CHUNKS, TOK, CW), bf16), vmem((CHUNKS, TOK, CW), bf16),
            vmem((CHUNKS, TOK, CW), bf16), dma((CHUNKS,)), dma((CHUNKS,)), dma((CHUNKS,)),
            dma((3,)), dma((3,)), dma((3,)),
            dma((NX - 1, NY)), dma((NX - 1, NY)), dma((NY - 1,)), dma((NY - 1,)), dma((NZ - 1,)), dma((NZ - 1,)),
            dma((NY - 1,)), dma((NY - 1,)), dma((NX - 1, NY)), dma((NX - 1, NY)), dma, dma,
            dma((CHUNKS,)), dma((CHUNKS,)),
        ],
        compiler_params=pltpu.CompilerParams(
            collective_id=0, has_side_effects=True, vmem_limit_bytes=60 * 1024 * 1024
        ),
    )(flora_seeds, plan, stashed.reshape(ROWS, D), kv_grads.reshape(MBW, TOK, 2 * KVW), branch_grads.reshape(TOK, D))
    return compressed.astype(f32)[None], grads[None]


def solution(mesh):
    placed = (
        P("pipe", None, "dp", None),
        P("pipe", None, "dp", None),
        P("pipe", "dp", None),
        P("pipe", None),
        P("pipe", None),
    )
    return jax.shard_map(
        per_device,
        mesh=mesh,
        in_specs=placed,
        out_specs=(P("pipe", None, None), P("pipe", "dp", None)),
        check_vma=False,
    )
```
